32 devices in a mesh: clip: 16 (over z, y, x), row: 2 (over core).
Axes of the slice: x: 2, y: 2, z: 4, core: 2. Of those that a mesh axis runs over, the one named last changes fastest.
Arguments:
- queries: bfloat16 [16, 512, 1792], P('clip', 'row'), may hold values from -36 to 36
- frames_kv: bfloat16 [16, 512, 512], P('clip', 'row'), may hold values from -20 to 20
- summary_kv: bfloat16 [16, 32, 512], P('clip', 'row'), may hold values from -6 to 6
- lengths: int32 [16], P('clip'), may hold values from 128 to 512, as said below
- caps: int32 [16], P('clip'), may hold values from 8 to 32, as said below
Outputs:
- attended: bfloat16 [16, 512, 1792], P('clip', 'row')
The draws below stay inside these ranges and needn't reach their ends.
Inputs may be any that keep to these rules, and one draw needn't show every extreme that they name: `lengths`: some clip of every draw has 512 frame tokens. `caps`: some clip of every draw keeps 32 summary tokens.
All inputs are finite; a program needn't handle non-finite values.
Results may differ from the reference program's by a relative error of at most 0.01.
Values may be sent and summed in bfloat16 or wider, within the bound.
A program may use at most 64 MiB of HBM per device.

```python
import jax
import jax.numpy as jnp
from jax import lax

HQ = 14
KVH = 2
HD = 128
WINDOW = 128
SLOTS = 32
TOK_CLIP = 512
CLIPS = 16


def paired_frames(key):
    base = jax.random.fold_in(key, 11)
    key_query, key_keys, key_values = jax.random.split(base, 3)
    group = HQ // KVH
    query_shape = (CLIPS, TOK_CLIP, KVH, group, HD)
    head_shape = (CLIPS, TOK_CLIP, KVH, HD)
    query = jax.random.truncated_normal(key_query, -6.0, 6.0, query_shape, jnp.float32)
    keys = jax.random.truncated_normal(key_keys, -6.0, 6.0, head_shape, jnp.float32)
    values = jax.random.truncated_normal(key_values, -6.0, 6.0, head_shape, jnp.float32)
    query = query.reshape(CLIPS, TOK_CLIP, HQ * HD)
    joined = jnp.concatenate([keys.reshape(CLIPS, TOK_CLIP, KVH * HD), values.reshape(CLIPS, TOK_CLIP, KVH * HD)], axis=-1)
    return (query, joined)


def draw_queries(key, part):
    query, joined = paired_frames(key)
    return query.astype(jnp.bfloat16)


def draw_frames_kv(key, part):
    query, joined = paired_frames(key)
    return joined.astype(jnp.bfloat16)


def draw_lengths(key, part):
    first, second = jax.random.split(jax.random.fold_in(key, 23))
    counts = jax.random.randint(first, (CLIPS,), TOK_CLIP // 4, TOK_CLIP + 1)
    chosen = jax.random.randint(second, (), 0, CLIPS)
    return counts.at[chosen].set(TOK_CLIP).astype(jnp.int32)


def draw_caps(key, part):
    first, second = jax.random.split(jax.random.fold_in(key, 37))
    counts = jax.random.randint(first, (CLIPS,), SLOTS // 4, SLOTS + 1)
    chosen = jax.random.randint(second, (), 0, CLIPS)
    return counts.at[chosen].set(SLOTS).astype(jnp.int32)


def levels(own_key, dims, shards, low, top_value):
    def one(position, shards_of):
        draws = jax.random.uniform(jax.random.fold_in(jax.random.fold_in(own_key, 6), position), (shards_of,), jnp.float32, low / len(shards), top_value / len(shards))
        return jnp.repeat(jnp.exp(draws), dims[position] // shards_of).reshape((-1,) + (1,) * (len(dims) - position - 1))

    gain = one(*shards[0])
    for cut in shards[1:]:
        gain = gain * one(*cut)
    return gain


def centred(rng, shape, deviation, bound, pieces=(), kind=jnp.bfloat16):
    values = deviation * jax.random.normal(rng, shape, jnp.float32)
    if pieces:
        values = values * levels(rng, shape, pieces, -0.22, 0.18)
    return jnp.clip(values, -bound, bound).astype(kind)


def setup_inputs(seed: int = 0) -> dict:
    arg_keys = jax.random.split(jax.random.key(seed), 6)
    return {
        "queries": draw_queries(jax.random.fold_in(arg_keys[5], 71), 0),
        "frames_kv": draw_frames_kv(jax.random.fold_in(arg_keys[5], 71), 0),
        "summary_kv": centred(arg_keys[2], (CLIPS, SLOTS, 2 * KVH * HD), 1.0, 6.0, ((0, 16), (1, 2))),
        "lengths": draw_lengths(jax.random.fold_in(arg_keys[5], 71), 0),
        "caps": draw_caps(jax.random.fold_in(arg_keys[5], 71), 0),
    }


def reference(queries, frames_kv, summary_kv, lengths, caps):
    group = HQ // KVH
    scale = HD ** -0.5
    positions = jnp.arange(TOK_CLIP)
    local_mask = (positions[None, :] <= positions[:, None]) & (positions[None, :] > positions[:, None] - WINDOW)
    summary_keys = summary_kv[:, :, :KVH * HD].reshape(CLIPS * SLOTS, KVH, HD).astype(jnp.float32)
    summary_values = summary_kv[:, :, KVH * HD:].reshape(CLIPS * SLOTS, KVH, HD)
    slot_live = (jnp.arange(SLOTS)[None, :] < caps[:, None]).reshape(-1)
    clip_of = jnp.repeat(jnp.arange(CLIPS), SLOTS)

    def one_clip(clip_now):
        query = queries[clip_now].reshape(TOK_CLIP, KVH, group, HD).astype(jnp.float32)
        frames = frames_kv[clip_now]
        keys = frames[:, :KVH * HD].reshape(TOK_CLIP, KVH, HD).astype(jnp.float32)
        values = frames[:, KVH * HD:].reshape(TOK_CLIP, KVH, HD)
        local = jnp.einsum('tkgd,skd->kgts', query, keys) * scale
        remote = jnp.einsum('tkgd,skd->kgts', query, summary_keys) * scale
        scores = jnp.concatenate([local, remote], axis=-1)
        remote_mask = jnp.broadcast_to((slot_live & (clip_of < clip_now))[None, :], (TOK_CLIP, CLIPS * SLOTS))
        mask = jnp.concatenate([local_mask, remote_mask], axis=-1)
        masked = jnp.where(mask, scores, -1e30)
        largest = jnp.max(masked, axis=-1, keepdims=True)
        weights = jnp.where(mask, jnp.exp(masked - largest), 0.0)
        total = jnp.sum(weights, axis=-1)
        every_value = jnp.concatenate([values, summary_values], axis=0).astype(jnp.float32)
        rounded = lax.optimization_barrier(weights.astype(jnp.bfloat16)).astype(jnp.float32)
        numer = jnp.einsum('kgts,skd->kgtd', rounded, every_value)
        result = numer / total[..., None]
        result = jnp.transpose(result, (2, 0, 1, 3)).reshape(TOK_CLIP, HQ * HD)
        result = jnp.where((positions < lengths[clip_now])[:, None], result, 0.0)
        return result.astype(jnp.bfloat16)

    return lax.map(one_clip, jnp.arange(CLIPS))
```

```python
import functools
import math

import jax
import jax.numpy as jnp
from jax import lax
from jax.experimental import pallas as pl
from jax.experimental.pallas import tpu as pltpu
from jax.sharding import PartitionSpec as P

KVH = 2
HD = 128
WINDOW = 128
MESH = pl.DeviceIdType.MESH
LOW = -1e30
DEAD = 1e30
EXP_SCALE = HD ** (-0.5) * math.log2(math.e)


def nt_dot(a, b):
    return lax.dot_general(a, b, (((1,), (1,)), ((), ())), preferred_element_type=jnp.float32)


def kernel(
    levels, group, heads,
    q_hbm, f_hbm, s_hbm, len_ref, cap_ref,
    out_ref,
    q, kv, raw, own, buf, acc, top,
    load_sem, a_send, a_recv, b_send, b_recv, c_send, c_recv, rim_send, rim_recv,
):
    tokens = q.shape[0]
    per_kv = heads // KVH
    half = own.shape[0]
    slots = 2 * half
    clip = lax.axis_index("clip")
    row = lax.axis_index("row")
    partner = 1 - row
    z = clip // group
    g = lax.rem(clip, group)
    blocks = tokens // WINDOW

    load_s = pltpu.make_async_copy(s_hbm, raw, load_sem.at[0])
    load_f = pltpu.make_async_copy(f_hbm, kv.at[pl.ds(WINDOW, tokens)], load_sem.at[1])
    load_q = pltpu.make_async_copy(q_hbm, q, load_sem.at[2])
    load_s.start()
    load_f.start()
    load_q.start()

    kw = KVH * HD
    buf[:, :, :, :kw] = jnp.zeros(buf.shape[:3] + (kw,), buf.dtype)
    buf[:, :, :, kw:] = jnp.full(buf.shape[:3] + (kw,), DEAD, buf.dtype)
    kv[:WINDOW] = jnp.zeros((WINDOW, kv.shape[1]), kv.dtype)

    barrier = pltpu.get_barrier_semaphore()
    pl.semaphore_signal(barrier, inc=1, device_id={"row": partner}, device_id_type=MESH)
    for zz in range(levels - 1):
        @pl.when(zz < z)
        def _():
            pl.semaphore_signal(barrier, inc=1, device_id={"clip": zz * group + g}, device_id_type=MESH)
    for gg in range(group):
        @pl.when((gg != g) & ((z > 0) | (gg < g)))
        def _():
            pl.semaphore_signal(barrier, inc=1, device_id={"clip": z * group + gg}, device_id_type=MESH)

    load_s.wait()
    slot_ids = row * half + lax.broadcasted_iota(jnp.int32, (half, kw), 0)
    own[:, :kw] = raw[:, :kw]
    own[:, kw:] = jnp.where(slot_ids < cap_ref[0], raw[:, kw:].astype(jnp.float32), DEAD).astype(own.dtype)

    count = 1 + (levels - 1 - z) + jnp.where(z > 0, group - 1, group - 1 - g)
    pl.semaphore_wait(barrier, count)

    def a_copy(src_z, dst_z):
        return pltpu.make_async_remote_copy(
            src_ref=own, dst_ref=buf.at[src_z * group + g, row],
            send_sem=a_send.at[dst_z], recv_sem=a_recv.at[src_z],
            device_id={"clip": dst_z * group + g}, device_id_type=MESH)

    def own_copy(gg):
        return pltpu.make_async_remote_copy(
            src_ref=own, dst_ref=buf.at[clip, row],
            send_sem=b_send.at[z * group + gg], recv_sem=b_recv.at[clip],
            device_id={"clip": z * group + gg}, device_id_type=MESH)

    def b_copy(p, gg):
        part = buf.at[p * group + g, row]
        return pltpu.make_async_remote_copy(
            src_ref=part, dst_ref=part,
            send_sem=b_send.at[p * group + gg], recv_sem=b_recv.at[p * group + g],
            device_id={"clip": z * group + gg}, device_id_type=MESH)

    def b_arrived(p, gg):
        part = buf.at[p * group + gg, row]
        pltpu.make_async_remote_copy(
            src_ref=part, dst_ref=part,
            send_sem=b_send.at[p * group + gg], recv_sem=b_recv.at[p * group + gg],
            device_id={"clip": z * group + gg}, device_id_type=MESH).wait_recv()

    def c_copy(p, side):
        part = buf.at[pl.ds(p * group, group), side]
        return pltpu.make_async_remote_copy(
            src_ref=part, dst_ref=part,
            send_sem=c_send.at[p], recv_sem=c_recv.at[p],
            device_id={"row": partner}, device_id_type=MESH)

    rim_copy = pltpu.make_async_remote_copy(
        src_ref=f_hbm.at[pl.ds(tokens - WINDOW, WINDOW)], dst_ref=kv.at[pl.ds(0, WINDOW)],
        send_sem=rim_send, recv_sem=rim_recv,
        device_id={"row": partner}, device_id_type=MESH)

    for zz in reversed(range(1, levels)):
        @pl.when(zz > z)
        def _():
            a_copy(z, zz).start()
    for gg in range(1, group):
        @pl.when(gg > g)
        def _():
            own_copy(gg).start()

    @pl.when(row == 0)
    def _():
        rim_copy.start()

    def stacked(k, j):
        rows = pl.ds(j * WINDOW, WINDOW)
        return jnp.concatenate(
            [q[rows, pl.ds((k * per_kv + i) * HD, HD)] for i in range(per_kv)], axis=0)

    ones = jnp.ones((2 * WINDOW, HD), jnp.bfloat16)

    def local(k, j):
        query = stacked(k, j)
        span = pl.ds(j * WINDOW, 2 * WINDOW)
        keys = kv[span, pl.ds(k * HD, HD)]
        values = jnp.concatenate([kv[span, pl.ds(kw + k * HD, HD)], ones], axis=1)
        t = lax.broadcasted_iota(jnp.int32, (WINDOW, 2 * WINDOW), 0)
        s = lax.broadcasted_iota(jnp.int32, (WINDOW, 2 * WINDOW), 1)
        near = (s > t) & (s <= t + WINDOW)
        if j == 0:
            near = near & (s >= jnp.where(row == 0, WINDOW, 0))
        bias = jnp.where(near, 0.0, LOW)
        scores = nt_dot(query, keys) + jnp.concatenate([bias] * per_kv, axis=0)
        largest = jnp.max(scores, axis=1, keepdims=True)
        weights = jnp.exp2((scores - largest) * EXP_SCALE).astype(jnp.bfloat16)
        unit = k * blocks + j
        acc[unit] = jnp.dot(weights, values, preferred_element_type=jnp.float32)
        top[unit] = jnp.broadcast_to(largest, top.shape[1:])

    load_f.wait()
    load_q.wait()
    for k in range(KVH):
        for j in range(1, blocks):
            local(k, j)

    for p in reversed(range(levels - 1)):
        @pl.when(p < z)
        def _():
            a_copy(p, z).wait_recv()
            for gg in range(group):
                @pl.when(gg != g)
                def _():
                    b_copy(p, gg).start()

    @pl.when(row == 1)
    def _():
        rim_copy.wait_recv()

    for k in range(KVH):
        local(k, 0)

    for p in reversed(range(levels)):
        @pl.when(p <= z)
        def _():
            for gg in range(group):
                @pl.when((gg != g) & ((p < z) | (gg < g)))
                def _():
                    b_arrived(p, gg)
            c_copy(p, row).start()

    for p in reversed(range(levels)):
        @pl.when(p <= z)
        def _():
            c_copy(p, partner).wait_recv()

    total = levels * group
    step = min(total, max(1, 512 // slots))
    first = (lax.broadcasted_iota(jnp.int32, (per_kv * WINDOW, HD), 1) == 0).astype(jnp.float32).astype(jnp.bfloat16)

    def remote(k, piece):
        part = pl.ds(piece * step, step)
        flat = (step * slots, HD)
        keys = buf[part, :, :, pl.ds(k * HD, HD)].reshape(flat)
        values = buf[part, :, :, pl.ds(kw + k * HD, HD)].reshape(flat).astype(jnp.float32)
        dead = values > 1e29
        keys = jnp.concatenate([keys, jnp.where(dead, LOW, 0.0).astype(jnp.bfloat16)], axis=1)
        values = jnp.where(dead, 0.0, values).astype(jnp.bfloat16)
        values = jnp.concatenate([values, jnp.ones(flat, jnp.bfloat16)], axis=1)
        for j in range(blocks):
            unit = k * blocks + j
            query = jnp.concatenate([stacked(k, j), first], axis=1)
            scores = nt_dot(query, keys)
            before = top[unit][:, :1]
            largest = jnp.maximum(before, jnp.max(scores, axis=1, keepdims=True))
            weights = jnp.exp2((scores - largest) * EXP_SCALE).astype(jnp.bfloat16)
            factor = jnp.exp2((before - largest) * EXP_SCALE)
            fresh = acc[unit] * factor + jnp.dot(weights, values, preferred_element_type=jnp.float32)
            acc[unit] = fresh
            if step < total:
                top[unit] = jnp.broadcast_to(largest, top.shape[1:])

    for k in range(KVH):
        if step == total:
            remote(k, 0)
        else:
            @pl.loop(0, total // step)
            def _(piece):
                remote(k, piece)
        for j in range(blocks):
            unit = k * blocks + j
            state = acc[unit]
            result = state[:, :HD] / state[:, HD:]
            pos = row * tokens + j * WINDOW + lax.broadcasted_iota(jnp.int32, (WINDOW, HD), 0)
            present = pos < len_ref[0]
            for i in range(per_kv):
                piece = result[i * WINDOW:(i + 1) * WINDOW]
                out_ref[pl.ds(j * WINDOW, WINDOW), pl.ds((k * per_kv + i) * HD, HD)] = (
                    jnp.where(present, piece, 0.0).astype(out_ref.dtype))

    for zz in range(1, levels):
        @pl.when(zz > z)
        def _():
            a_copy(z, zz).wait_send()
    for gg in range(1, group):
        @pl.when(gg > g)
        def _():
            own_copy(gg).wait_send()
    for p in range(levels - 1):
        @pl.when(p < z)
        def _():
            for gg in range(group):
                @pl.when(gg != g)
                def _():
                    b_copy(p, gg).wait_send()
    for p in range(levels):
        @pl.when(p <= z)
        def _():
            c_copy(p, row).wait_send()

    @pl.when(row == 0)
    def _():
        rim_copy.wait_send()


def shards(clips, queries, frames_kv, summary_kv, lengths, caps):
    tokens, width = queries.shape[1:]
    half, kv_width = summary_kv.shape[1:]
    heads = width // HD
    group = 1
    while group * group * 4 <= clips and clips % (group * 2) == 0:
        group *= 2
    levels = clips // group
    units = KVH * (tokens // WINDOW)
    rows = heads // KVH * WINDOW
    dma = pltpu.SemaphoreType.DMA
    anywhere = pl.BlockSpec(memory_space=pl.ANY)
    scalar = pl.BlockSpec(memory_space=pltpu.SMEM)
    out = pl.pallas_call(
        functools.partial(kernel, levels, group, heads),
        out_shape=jax.ShapeDtypeStruct((tokens, width), jnp.bfloat16),
        in_specs=[anywhere, anywhere, anywhere, scalar, scalar],
        out_specs=pl.BlockSpec(memory_space=pltpu.VMEM),
        scratch_shapes=[
            pltpu.VMEM((tokens, width), jnp.bfloat16),
            pltpu.VMEM((WINDOW + tokens, kv_width), jnp.bfloat16),
            pltpu.VMEM((half, kv_width), jnp.bfloat16),
            pltpu.VMEM((half, kv_width), jnp.bfloat16),
            pltpu.VMEM((clips, 2, half, kv_width), jnp.bfloat16),
            pltpu.VMEM((units, rows, 2 * HD), jnp.float32),
            pltpu.VMEM((units, rows, HD), jnp.float32),
            dma((3,)),
            dma((levels,)), dma((levels,)),
            dma((clips,)), dma((clips,)),
            dma((levels,)), dma((levels,)),
            dma, dma,
        ],
        compiler_params=pltpu.CompilerParams(
            collective_id=0, has_side_effects=True, vmem_limit_bytes=48 * 2**20),
    )(queries[0], frames_kv[0], summary_kv[0], lengths, caps)
    return out[None]


def solution(mesh):
    placed = (
        P("clip", "row", None),
        P("clip", "row", None),
        P("clip", "row", None),
        P("clip"),
        P("clip"),
    )
    return jax.shard_map(
        functools.partial(shards, mesh.shape["clip"]),
        mesh=mesh, in_specs=placed, out_specs=P("clip", "row", None), check_vma=False
    )
```

```python
import functools
import math

import jax
import jax.numpy as jnp
from jax import lax
from jax.experimental import pallas as pl
from jax.experimental.pallas import tpu as pltpu
from jax.sharding import PartitionSpec as P

KVH = 2
HD = 128
WINDOW = 128
CHUNK = 32
MESH = pl.DeviceIdType.MESH
LOW = -1e30
DEAD = 1e30
EXP_SCALE = HD ** (-0.5) * math.log2(math.e)


def nt_dot(a, b):
    return lax.dot_general(a, b, (((1,), (1,)), ((), ())), preferred_element_type=jnp.float32)


def kernel(
    levels, group, heads,
    q_hbm, f_hbm, s_hbm, len_ref, cap_ref,
    out_ref,
    q, kv, raw, own, buf, acc, top, scores, rounded, factor, near_bias,
    load_sem, a_send, a_recv, b_send, b_recv, c_send, c_recv, rim_send, rim_recv,
):
    tokens = q.shape[0]
    per_kv = heads // KVH
    half = own.shape[0]
    slots = 2 * half
    clip = lax.axis_index("clip")
    row = lax.axis_index("row")
    partner = 1 - row
    z = clip // group
    g = lax.rem(clip, group)
    blocks = tokens // WINDOW

    load_s = pltpu.make_async_copy(s_hbm, raw, load_sem.at[0])
    load_f = pltpu.make_async_copy(f_hbm, kv.at[pl.ds(WINDOW, tokens)], load_sem.at[1])
    load_q = pltpu.make_async_copy(q_hbm, q, load_sem.at[2])
    load_s.start()
    load_f.start()
    load_q.start()

    kw = KVH * HD
    buf[:, :, :, :kw] = jnp.zeros(buf.shape[:3] + (kw,), buf.dtype)
    buf[:, :, :, kw:] = jnp.full(buf.shape[:3] + (kw,), DEAD, buf.dtype)
    kv[:WINDOW] = jnp.zeros((WINDOW, kv.shape[1]), kv.dtype)

    barrier = pltpu.get_barrier_semaphore()
    pl.semaphore_signal(barrier, inc=1, device_id={"row": partner}, device_id_type=MESH)
    for zz in range(levels - 1):
        @pl.when(zz < z)
        def _():
            pl.semaphore_signal(barrier, inc=1, device_id={"clip": zz * group + g}, device_id_type=MESH)
    for gg in range(group):
        @pl.when((gg != g) & ((z > 0) | (gg < g)))
        def _():
            pl.semaphore_signal(barrier, inc=1, device_id={"clip": z * group + gg}, device_id_type=MESH)

    load_s.wait()
    slot_ids = row * half + lax.broadcasted_iota(jnp.int32, (half, kw), 0)
    own[:, :kw] = raw[:, :kw]
    own[:, kw:] = jnp.where(slot_ids < cap_ref[0], raw[:, kw:].astype(jnp.float32), DEAD).astype(own.dtype)

    count = 1 + (levels - 1 - z) + jnp.where(z > 0, group - 1, group - 1 - g)
    pl.semaphore_wait(barrier, count)

    def a_copy(src_z, dst_z):
        return pltpu.make_async_remote_copy(
            src_ref=own, dst_ref=buf.at[src_z * group + g, row],
            send_sem=a_send.at[dst_z], recv_sem=a_recv.at[src_z],
            device_id={"clip": dst_z * group + g}, device_id_type=MESH)

    def own_copy(gg):
        return pltpu.make_async_remote_copy(
            src_ref=own, dst_ref=buf.at[clip, row],
            send_sem=b_send.at[z * group + gg], recv_sem=b_recv.at[clip],
            device_id={"clip": z * group + gg}, device_id_type=MESH)

    def b_copy(p, gg):
        part = buf.at[p * group + g, row]
        return pltpu.make_async_remote_copy(
            src_ref=part, dst_ref=part,
            send_sem=b_send.at[p * group + gg], recv_sem=b_recv.at[p * group + g],
            device_id={"clip": z * group + gg}, device_id_type=MESH)

    def b_arrived(p, gg):
        part = buf.at[p * group + gg, row]
        pltpu.make_async_remote_copy(
            src_ref=part, dst_ref=part,
            send_sem=b_send.at[p * group + gg], recv_sem=b_recv.at[p * group + gg],
            device_id={"clip": z * group + gg}, device_id_type=MESH).wait_recv()

    def c_copy(p, side):
        part = buf.at[pl.ds(p * group, group), side]
        return pltpu.make_async_remote_copy(
            src_ref=part, dst_ref=part,
            send_sem=c_send.at[p], recv_sem=c_recv.at[p],
            device_id={"row": partner}, device_id_type=MESH)

    rim_copy = pltpu.make_async_remote_copy(
        src_ref=f_hbm.at[pl.ds(tokens - WINDOW, WINDOW)], dst_ref=kv.at[pl.ds(0, WINDOW)],
        send_sem=rim_send, recv_sem=rim_recv,
        device_id={"row": partner}, device_id_type=MESH)

    for zz in reversed(range(1, levels)):
        @pl.when(zz > z)
        def _():
            a_copy(z, zz).start()
    for gg in range(1, group):
        @pl.when(gg > g)
        def _():
            own_copy(gg).start()

    @pl.when(row == 0)
    def _():
        rim_copy.start()

    def stacked(k, j):
        rows = pl.ds(j * WINDOW, WINDOW)
        return jnp.concatenate(
            [q[rows, pl.ds((k * per_kv + i) * HD, HD)] for i in range(per_kv)], axis=0)

    rows = per_kv * WINDOW
    wide = 2 * WINDOW
    ones = jnp.ones((wide, HD), jnp.bfloat16)

    def twice(x):
        return jnp.concatenate([x, x], axis=1)

    def attend(unit, query, keys, values, bias, start):
        scores[unit] = nt_dot(query, keys)
        for r in range(0, rows, CHUNK):
            part = pl.ds(r, CHUNK)
            s = scores[unit, part]
            if bias is not None:
                s = s + bias[pl.ds(r % WINDOW, CHUNK)]
            largest = jnp.maximum(s[:, :HD], s[:, HD:])
            largest = jnp.broadcast_to(jnp.max(largest, axis=1, keepdims=True), (CHUNK, HD))
            if not start:
                before = top[unit, part]
                largest = jnp.maximum(before, largest)
                factor[unit, part] = jnp.exp2((before - largest) * EXP_SCALE)
            top[unit, part] = largest
            rounded[unit, part] = jnp.exp2((s - twice(largest)) * EXP_SCALE).astype(jnp.bfloat16)
        fresh = jnp.dot(rounded[unit], values, preferred_element_type=jnp.float32)
        if start:
            acc[unit] = fresh
        else:
            for r in range(0, rows, CHUNK):
                part = pl.ds(r, CHUNK)
                acc[unit, part] = acc[unit, part] * twice(factor[unit, part]) + fresh[r:r + CHUNK]

    t = lax.broadcasted_iota(jnp.int32, (WINDOW, wide), 0)
    s = lax.broadcasted_iota(jnp.int32, (WINDOW, wide), 1)
    near = (s > t) & (s <= t + WINDOW)
    near_bias[1] = jnp.where(near, 0.0, LOW)
    near_bias[0] = jnp.where(near & (s >= jnp.where(row == 0, WINDOW, 0)), 0.0, LOW)

    def local(k, j):
        span = pl.ds(j * WINDOW, wide)
        keys = kv[span, pl.ds(k * HD, HD)]
        values = jnp.concatenate([kv[span, pl.ds(kw + k * HD, HD)], ones], axis=1)
        attend(k * blocks + j, stacked(k, j), keys, values, near_bias.at[min(j, 1)], True)

    load_f.wait()
    load_q.wait()
    for k in range(KVH):
        for j in range(1, blocks):
            local(k, j)

    for p in reversed(range(levels - 1)):
        @pl.when(p < z)
        def _():
            a_copy(p, z).wait_recv()
            for gg in range(group):
                @pl.when(gg != g)
                def _():
                    b_copy(p, gg).start()

    @pl.when(row == 1)
    def _():
        rim_copy.wait_recv()

    for k in range(KVH):
        local(k, 0)

    first = (lax.broadcasted_iota(jnp.int32, (rows, HD), 1) == 0).astype(jnp.float32).astype(jnp.bfloat16)
    step = wide // slots
    assert step % group == 0 or group % step == 0

    def remote(piece):
        part = pl.ds(piece * step, step)
        for k in range(KVH):
            keys = buf[part, :, :, pl.ds(k * HD, HD)].reshape(wide, HD)
            values = buf[part, :, :, pl.ds(kw + k * HD, HD)].reshape(wide, HD).astype(jnp.float32)
            dead = values > 1e29
            keys = jnp.concatenate([keys, jnp.where(dead, LOW, 0.0).astype(jnp.bfloat16)], axis=1)
            values = jnp.concatenate([jnp.where(dead, 0.0, values).astype(jnp.bfloat16), ones], axis=1)
            for j in range(blocks):
                query = jnp.concatenate([stacked(k, j), first], axis=1)
                attend(k * blocks + j, query, keys, values, None, False)

    per_piece = max(1, step // group)
    for high in reversed(range(0, levels, per_piece)):
        @pl.when(high <= z)
        def _():
            for p in reversed(range(high, min(high + per_piece, levels))):
                @pl.when(p <= z)
                def _():
                    for gg in range(group):
                        @pl.when((gg != g) & ((p < z) | (gg < g)))
                        def _():
                            b_arrived(p, gg)
                    c_copy(p, row).start()

    for high in reversed(range(0, levels, per_piece)):
        @pl.when(high <= z)
        def _():
            for p in reversed(range(high, min(high + per_piece, levels))):
                @pl.when(p <= z)
                def _():
                    c_copy(p, partner).wait_recv()
            pieces = max(1, group // step)
            if pieces == 1:
                remote(high // per_piece)
            else:
                @pl.loop(0, pieces)
                def _(i):
                    remote(high * pieces + i)

    for k in range(KVH):
        for j in range(blocks):
            unit = k * blocks + j
            pos = row * tokens + j * WINDOW + lax.broadcasted_iota(jnp.int32, (WINDOW, HD), 0)
            present = pos < len_ref[0]
            for i in range(per_kv):
                part = pl.ds(i * WINDOW, WINDOW)
                result = acc[unit, part, pl.ds(0, HD)] / acc[unit, part, pl.ds(HD, HD)]
                out_ref[pl.ds(j * WINDOW, WINDOW), pl.ds((k * per_kv + i) * HD, HD)] = (
                    jnp.where(present, result, 0.0).astype(out_ref.dtype))

    for zz in range(1, levels):
        @pl.when(zz > z)
        def _():
            a_copy(z, zz).wait_send()
    for gg in range(1, group):
        @pl.when(gg > g)
        def _():
            own_copy(gg).wait_send()
    for p in range(levels - 1):
        @pl.when(p < z)
        def _():
            for gg in range(group):
                @pl.when(gg != g)
                def _():
                    b_copy(p, gg).wait_send()
    for p in range(levels):
        @pl.when(p <= z)
        def _():
            c_copy(p, row).wait_send()

    @pl.when(row == 0)
    def _():
        rim_copy.wait_send()


def shards(clips, queries, frames_kv, summary_kv, lengths, caps):
    tokens, width = queries.shape[1:]
    half, kv_width = summary_kv.shape[1:]
    heads = width // HD
    group = 1
    while group * group * 4 <= clips and clips % (group * 2) == 0:
        group *= 2
    levels = clips // group
    units = KVH * (tokens // WINDOW)
    rows = heads // KVH * WINDOW
    dma = pltpu.SemaphoreType.DMA
    anywhere = pl.BlockSpec(memory_space=pl.ANY)
    scalar = pl.BlockSpec(memory_space=pltpu.SMEM)
    out = pl.pallas_call(
        functools.partial(kernel, levels, group, heads),
        out_shape=jax.ShapeDtypeStruct((tokens, width), jnp.bfloat16),
        in_specs=[anywhere, anywhere, anywhere, scalar, scalar],
        out_specs=pl.BlockSpec(memory_space=pltpu.VMEM),
        scratch_shapes=[
            pltpu.VMEM((tokens, width), jnp.bfloat16),
            pltpu.VMEM((WINDOW + tokens, kv_width), jnp.bfloat16),
            pltpu.VMEM((half, kv_width), jnp.bfloat16),
            pltpu.VMEM((half, kv_width), jnp.bfloat16),
            pltpu.VMEM((clips, 2, half, kv_width), jnp.bfloat16),
            pltpu.VMEM((units, rows, 2 * HD), jnp.float32),
            pltpu.VMEM((units, rows, HD), jnp.float32),
            pltpu.VMEM((units, rows, 2 * WINDOW), jnp.float32),
            pltpu.VMEM((units, rows, 2 * WINDOW), jnp.bfloat16),
            pltpu.VMEM((units, rows, HD), jnp.float32),
            pltpu.VMEM((2, WINDOW, 2 * WINDOW), jnp.float32),
            dma((3,)),
            dma((levels,)), dma((levels,)),
            dma((clips,)), dma((clips,)),
            dma((levels,)), dma((levels,)),
            dma, dma,
        ],
        compiler_params=pltpu.CompilerParams(
            collective_id=0, has_side_effects=True, vmem_limit_bytes=48 * 2**20),
    )(*[pltpu.with_memory_space_constraint(x[0], pltpu.HBM) for x in (queries, frames_kv, summary_kv)], lengths, caps)
    return out[None]


def solution(mesh):
    placed = (
        P("clip", "row", None),
        P("clip", "row", None),
        P("clip", "row", None),
        P("clip"),
        P("clip"),
    )
    return jax.shard_map(
        functools.partial(shards, mesh.shape["clip"]),
        mesh=mesh, in_specs=placed, out_specs=P("clip", "row", None), check_vma=False
    )
```

```python
import functools
import math

import jax
import jax.numpy as jnp
from jax import lax
from jax.experimental import pallas as pl
from jax.experimental.pallas import tpu as pltpu
from jax.sharding import PartitionSpec as P

KVH = 2
HD = 128
WINDOW = 128
CHUNK = 32
MESH = pl.DeviceIdType.MESH
LOW = -1e30
DEAD = 1e30
EXP_SCALE = HD ** (-0.5) * math.log2(math.e)


def each(low, high, act):
    if high - low <= 4:
        for i in range(low, high):
            act(i)
    else:
        pl.loop(low, high)(act)


def nt_dot(a, b):
    return lax.dot_general(a, b, (((1,), (1,)), ((), ())), preferred_element_type=jnp.float32)


def kernel(
    levels, group, heads,
    q_hbm, f_hbm, s_hbm, len_hbm, cap_hbm,
    out_ref,
    len_ref, cap_ref, q, kv, raw, own, buf, acc, top, scores, rounded, factor, near_bias,
    load_sem, up_send, up_recv, in_send, in_recv, rim_send, rim_recv,
):
    tokens = q.shape[0]
    per_kv = heads // KVH
    half = own.shape[0]
    slots = 2 * half
    clip = lax.axis_index("clip")
    row = lax.axis_index("row")
    partner = 1 - row
    z = clip // group
    g = lax.rem(clip, group)
    blocks = tokens // WINDOW

    load_s = pltpu.make_async_copy(s_hbm, raw, load_sem.at[0])
    load_f = pltpu.make_async_copy(f_hbm, kv.at[pl.ds(WINDOW, tokens)], load_sem.at[1])
    load_q = pltpu.make_async_copy(q_hbm, q, load_sem.at[2])
    load_len = pltpu.make_async_copy(len_hbm, len_ref, load_sem.at[3])
    load_cap = pltpu.make_async_copy(cap_hbm, cap_ref, load_sem.at[4])
    load_s.start()
    load_cap.start()
    load_len.start()
    load_f.start()
    load_q.start()

    kw = KVH * HD
    buf[:, :, :, :kw] = jnp.zeros(buf.shape[:3] + (kw,), buf.dtype)
    buf[:, :, :, kw:] = jnp.full(buf.shape[:3] + (kw,), DEAD, buf.dtype)
    kv[:WINDOW] = jnp.zeros((WINDOW, kv.shape[1]), kv.dtype)

    barrier = pltpu.get_barrier_semaphore()
    pl.semaphore_signal(barrier, inc=1, device_id={"row": partner}, device_id_type=MESH)

    @pl.when(z > 0)
    def _():
        pl.semaphore_signal(barrier, inc=1, device_id={"clip": clip - group}, device_id_type=MESH)
    def greet(gg):
        @pl.when((gg != g) & ((z > 0) | (gg < g)))
        def _():
            for side in range(2):
                pl.semaphore_signal(
                    barrier, inc=1, device_id={"clip": z * group + gg, "row": side}, device_id_type=MESH)

    each(0, group, greet)

    load_s.wait()
    load_cap.wait()
    slot_ids = row * half + lax.broadcasted_iota(jnp.int32, (half, kw), 0)
    own[:, :kw] = raw[:, :kw]
    own[:, kw:] = jnp.where(slot_ids < cap_ref[0], raw[:, kw:].astype(jnp.float32), DEAD).astype(own.dtype)

    above = jnp.where(z < levels - 1, 1, 0)
    pl.semaphore_wait(barrier, 1 + above + 2 * jnp.where(z > 0, group - 1, group - 1 - g))

    def up(src, p):
        return pltpu.make_async_remote_copy(
            src_ref=src, dst_ref=buf.at[p * group + g, row],
            send_sem=up_send.at[p], recv_sem=up_recv.at[p],
            device_id={"clip": clip + group}, device_id_type=MESH)

    def up_arrived(p):
        part = buf.at[p * group + g, row]
        pltpu.make_async_remote_copy(
            src_ref=part, dst_ref=part, send_sem=up_send.at[p], recv_sem=up_recv.at[p],
            device_id={"clip": clip - group}, device_id_type=MESH).wait_recv()

    def across(src, p, gg, side):
        block = p * group + g
        return pltpu.make_async_remote_copy(
            src_ref=src, dst_ref=buf.at[block, row],
            send_sem=in_send.at[p * group + gg, side], recv_sem=in_recv.at[block, row],
            device_id={"clip": z * group + gg, "row": side}, device_id_type=MESH)

    def across_arrived(p, gg, side):
        part = buf.at[p * group + gg, side]
        pltpu.make_async_remote_copy(
            src_ref=part, dst_ref=part,
            send_sem=in_send.at[p * group + gg, side], recv_sem=in_recv.at[p * group + gg, side],
            device_id={"row": partner}, device_id_type=MESH).wait_recv()

    def forward(p):
        part = buf.at[p * group + g, row]

        @pl.when(z < levels - 1)
        def _():
            up(part, p).start()

        def hand(gg):
            @pl.when(gg != g)
            def _():
                for side in range(2):
                    across(part, p, gg, side).start()

        each(0, group, hand)
        across(part, p, g, partner).start()

    rim_copy = pltpu.make_async_remote_copy(
        src_ref=f_hbm.at[pl.ds(tokens - WINDOW, WINDOW)], dst_ref=kv.at[pl.ds(0, WINDOW)],
        send_sem=rim_send, recv_sem=rim_recv,
        device_id={"row": partner}, device_id_type=MESH)

    @pl.when(z < levels - 1)
    def _():
        up(own, z).start()

    def hand_own(gg):
        @pl.when(gg > g)
        def _():
            for side in range(2):
                across(own, z, gg, side).start()

    each(1, group, hand_own)

    @pl.when(row == 0)
    def _():
        rim_copy.start()

    def stacked(k, j):
        rows = pl.ds(j * WINDOW, WINDOW)
        return jnp.concatenate(
            [q[rows, pl.ds((k * per_kv + i) * HD, HD)] for i in range(per_kv)], axis=0)

    rows = per_kv * WINDOW
    wide = 2 * WINDOW
    ones = jnp.ones((wide, HD), jnp.bfloat16)

    def twice(x):
        return jnp.concatenate([x, x], axis=1)

    def attend(unit, query, keys, values, bias, start):
        scores[unit] = nt_dot(query, keys)
        for r in range(0, rows, CHUNK):
            part = pl.ds(r, CHUNK)
            s = scores[unit, part]
            if bias is not None:
                s = s + bias[pl.ds(r % WINDOW, CHUNK)]
            largest = jnp.maximum(s[:, :HD], s[:, HD:])
            largest = jnp.broadcast_to(jnp.max(largest, axis=1, keepdims=True), (CHUNK, HD))
            if not start:
                before = top[unit, part]
                largest = jnp.maximum(before, largest)
                factor[unit, part] = jnp.exp2((before - largest) * EXP_SCALE)
            top[unit, part] = largest
            rounded[unit, part] = jnp.exp2((s - twice(largest)) * EXP_SCALE).astype(jnp.bfloat16)
        fresh = jnp.dot(rounded[unit], values, preferred_element_type=jnp.float32)
        if start:
            acc[unit] = fresh
        else:
            for r in range(0, rows, CHUNK):
                part = pl.ds(r, CHUNK)
                acc[unit, part] = acc[unit, part] * twice(factor[unit, part]) + fresh[r:r + CHUNK]

    t = lax.broadcasted_iota(jnp.int32, (WINDOW, wide), 0)
    s = lax.broadcasted_iota(jnp.int32, (WINDOW, wide), 1)
    near = (s > t) & (s <= t + WINDOW)
    near_bias[1] = jnp.where(near, 0.0, LOW)
    near_bias[0] = jnp.where(near & (s >= jnp.where(row == 0, WINDOW, 0)), 0.0, LOW)

    def local(k, j):
        span = pl.ds(j * WINDOW, wide)
        keys = kv[span, pl.ds(k * HD, HD)]
        values = jnp.concatenate([kv[span, pl.ds(kw + k * HD, HD)], ones], axis=1)
        attend(k * blocks + j, stacked(k, j), keys, values, near_bias.at[min(j, 1)], True)

    load_f.wait()
    load_q.wait()
    load_len.wait()
    for k in range(KVH):
        for j in range(1, blocks):
            local(k, j)

    def relay(back):
        @pl.when(z >= back)
        def _():
            up_arrived(z - back)
            forward(z - back)

    relay(1)

    @pl.when(row == 1)
    def _():
        rim_copy.wait_recv()

    for k in range(KVH):
        local(k, 0)

    each(2, levels, relay)

    first = (lax.broadcasted_iota(jnp.int32, (rows, HD), 1) == 0).astype(jnp.float32).astype(jnp.bfloat16)
    step = wide // slots
    assert slots * step == wide and (step % group == 0 or group % step == 0)

    def remote(piece):
        part = pl.ds(piece * step, step)
        for k in range(KVH):
            keys = buf[part, :, :, pl.ds(k * HD, HD)].reshape(wide, HD)
            values = buf[part, :, :, pl.ds(kw + k * HD, HD)].reshape(wide, HD).astype(jnp.float32)
            dead = values > 1e29
            keys = jnp.concatenate([keys, jnp.where(dead, LOW, 0.0).astype(jnp.bfloat16)], axis=1)
            values = jnp.concatenate([jnp.where(dead, 0.0, values).astype(jnp.bfloat16), ones], axis=1)
            for j in range(blocks):
                query = jnp.concatenate([stacked(k, j), first], axis=1)
                attend(k * blocks + j, query, keys, values, None, False)

    per_piece = max(1, step // group)
    assert levels % per_piece == 0
    pieces = max(1, group // step)

    def take(i):
        high = (levels // per_piece - 1 - i) * per_piece

        @pl.when(high <= z)
        def _():
            def arrive(p):
                @pl.when(p <= z)
                def _():
                    def block(gg):
                        @pl.when((gg != g) & ((p < z) | (gg < g)))
                        def _():
                            for side in range(2):
                                across_arrived(p, gg, side)

                    each(0, group, block)

                @pl.when(p < z)
                def _():
                    across_arrived(p, g, partner)

            for p in reversed(range(per_piece)):
                arrive(high + p)
            if pieces == 1:
                remote(high // per_piece)
            else:
                @pl.loop(0, pieces)
                def _(i):
                    remote(high * pieces + i)

    each(0, levels // per_piece, take)

    for k in range(KVH):
        for j in range(blocks):
            unit = k * blocks + j
            pos = row * tokens + j * WINDOW + lax.broadcasted_iota(jnp.int32, (WINDOW, HD), 0)
            present = pos < len_ref[0]
            for i in range(per_kv):
                part = pl.ds(i * WINDOW, WINDOW)
                result = acc[unit, part, pl.ds(0, HD)] / acc[unit, part, pl.ds(HD, HD)]
                out_ref[pl.ds(j * WINDOW, WINDOW), pl.ds((k * per_kv + i) * HD, HD)] = (
                    jnp.where(present, result, 0.0).astype(out_ref.dtype))

    @pl.when(z < levels - 1)
    def _():
        up(own, z).wait_send()

    def left_own(gg):
        @pl.when(gg > g)
        def _():
            for side in range(2):
                across(own, z, gg, side).wait_send()

    each(1, group, left_own)

    def left(p):
        @pl.when(p < z)
        def _():
            part = buf.at[p * group + g, row]

            @pl.when(z < levels - 1)
            def _():
                up(part, p).wait_send()

            def gone(gg):
                @pl.when(gg != g)
                def _():
                    for side in range(2):
                        across(part, p, gg, side).wait_send()

            each(0, group, gone)
            across(part, p, g, partner).wait_send()

    each(0, levels - 1, left)

    @pl.when(row == 0)
    def _():
        rim_copy.wait_send()


def shards(clips, queries, frames_kv, summary_kv, lengths, caps):
    tokens, width = queries.shape[1:]
    half, kv_width = summary_kv.shape[1:]
    heads = width // HD
    group = 1
    while group * group * 4 <= clips and clips % (group * 2) == 0:
        group *= 2
    levels = clips // group
    units = KVH * (tokens // WINDOW)
    rows = heads // KVH * WINDOW
    dma = pltpu.SemaphoreType.DMA
    anywhere = pl.BlockSpec(memory_space=pl.ANY)
    out = pl.pallas_call(
        functools.partial(kernel, levels, group, heads),
        out_shape=jax.ShapeDtypeStruct((tokens, width), jnp.bfloat16),
        in_specs=[anywhere] * 3 + [pl.BlockSpec(memory_space=pltpu.HBM)] * 2,
        out_specs=pl.BlockSpec(memory_space=pltpu.VMEM),
        scratch_shapes=[
            pltpu.SMEM((1,), jnp.int32),
            pltpu.SMEM((1,), jnp.int32),
            pltpu.VMEM((tokens, width), jnp.bfloat16),
            pltpu.VMEM((WINDOW + tokens, kv_width), jnp.bfloat16),
            pltpu.VMEM((half, kv_width), jnp.bfloat16),
            pltpu.VMEM((half, kv_width), jnp.bfloat16),
            pltpu.VMEM((clips, 2, half, kv_width), jnp.bfloat16),
            pltpu.VMEM((units, rows, 2 * HD), jnp.float32),
            pltpu.VMEM((units, rows, HD), jnp.float32),
            pltpu.VMEM((units, rows, 2 * WINDOW), jnp.float32),
            pltpu.VMEM((units, rows, 2 * WINDOW), jnp.bfloat16),
            pltpu.VMEM((units, rows, HD), jnp.float32),
            pltpu.VMEM((2, WINDOW, 2 * WINDOW), jnp.float32),
            dma((5,)),
            dma((levels,)), dma((levels,)),
            dma((clips, 2)), dma((clips, 2)),
            dma, dma,
        ],
        compiler_params=pltpu.CompilerParams(
            collective_id=0, has_side_effects=True, vmem_limit_bytes=48 * 2**20),
    )(*[pltpu.with_memory_space_constraint(x[0], pltpu.HBM)
        for x in (queries, frames_kv, summary_kv)], lengths, caps)
    return out[None]


def solution(mesh):
    placed = (
        P("clip", "row", None),
        P("clip", "row", None),
        P("clip", "row", None),
        P("clip"),
        P("clip"),
    )
    return jax.shard_map(
        functools.partial(shards, mesh.shape["clip"]),
        mesh=mesh, in_specs=placed, out_specs=P("clip", "row", None), check_vma=False
    )
```

```python
import functools
import math

import jax
import jax.numpy as jnp
from jax import lax
from jax.experimental import pallas as pl
from jax.experimental.pallas import tpu as pltpu
from jax.sharding import PartitionSpec as P

KVH = 2
HD = 128
WINDOW = 128
CHUNK = 32
MESH = pl.DeviceIdType.MESH
LOW = -1e30
DEAD = 1e30
EXP_SCALE = HD ** (-0.5) * math.log2(math.e)


def each(low, high, act):
    if high - low <= 4:
        for i in range(low, high):
            act(i)
    else:
        pl.loop(low, high)(act)


def nt_dot(a, b):
    return lax.dot_general(a, b, (((1,), (1,)), ((), ())), preferred_element_type=jnp.float32)


def kernel(
    levels, group, heads,
    q_hbm, f_hbm, s_hbm, len_hbm, cap_hbm,
    out_ref,
    len_ref, cap_ref, q, kv, raw, own, buf, acc, top, scores, rounded, factor, near_bias,
    load_sem, up_send, up_recv, in_send, in_recv, rim_send, rim_recv,
):
    tokens = q.shape[0]
    per_kv = heads // KVH
    half = own.shape[0]
    slots = 2 * half
    clip = lax.axis_index("clip")
    row = lax.axis_index("row")
    partner = 1 - row
    z = clip // group
    g = lax.rem(clip, group)
    blocks = tokens // WINDOW

    load_s = pltpu.make_async_copy(s_hbm, raw, load_sem.at[0])
    load_f = pltpu.make_async_copy(f_hbm, kv.at[pl.ds(WINDOW, tokens)], load_sem.at[1])
    load_q = pltpu.make_async_copy(q_hbm, q, load_sem.at[2])
    load_len = pltpu.make_async_copy(len_hbm, len_ref, load_sem.at[3])
    load_cap = pltpu.make_async_copy(cap_hbm, cap_ref, load_sem.at[4])
    load_s.start()
    load_cap.start()
    load_len.start()
    load_f.start()
    load_q.start()

    kw = KVH * HD
    buf[:, :, :, :kw] = jnp.zeros(buf.shape[:3] + (kw,), buf.dtype)
    buf[:, :, :, kw:] = jnp.full(buf.shape[:3] + (kw,), DEAD, buf.dtype)
    kv[:WINDOW] = jnp.zeros((WINDOW, kv.shape[1]), kv.dtype)

    barrier = pltpu.get_barrier_semaphore()
    pl.semaphore_signal(barrier, inc=1, device_id={"row": partner}, device_id_type=MESH)

    def greet_below(zz):
        @pl.when(zz < z)
        def _():
            pl.semaphore_signal(barrier, inc=1, device_id={"clip": zz * group + g}, device_id_type=MESH)

    each(0, levels - 1, greet_below)
    def greet(gg):
        @pl.when((gg != g) & ((z > 0) | (gg < g)))
        def _():
            for side in range(2):
                pl.semaphore_signal(
                    barrier, inc=1, device_id={"clip": z * group + gg, "row": side}, device_id_type=MESH)

    each(0, group, greet)

    load_s.wait()
    load_cap.wait()
    slot_ids = row * half + lax.broadcasted_iota(jnp.int32, (half, kw), 0)
    own[:, :kw] = raw[:, :kw]
    own[:, kw:] = jnp.where(slot_ids < cap_ref[0], raw[:, kw:].astype(jnp.float32), DEAD).astype(own.dtype)

    pl.semaphore_wait(barrier, levels - z + 2 * jnp.where(z > 0, group - 1, group - 1 - g))

    def up(zz):
        return pltpu.make_async_remote_copy(
            src_ref=own, dst_ref=buf.at[clip, row],
            send_sem=up_send.at[zz], recv_sem=up_recv.at[z],
            device_id={"clip": zz * group + g}, device_id_type=MESH)

    def up_arrived(p):
        part = buf.at[p * group + g, row]
        pltpu.make_async_remote_copy(
            src_ref=part, dst_ref=part, send_sem=up_send.at[p], recv_sem=up_recv.at[p],
            device_id={"clip": p * group + g}, device_id_type=MESH).wait_recv()

    def across(src, p, gg, side):
        block = p * group + g
        return pltpu.make_async_remote_copy(
            src_ref=src, dst_ref=buf.at[block, row],
            send_sem=in_send.at[p * group + gg, side], recv_sem=in_recv.at[block, row],
            device_id={"clip": z * group + gg, "row": side}, device_id_type=MESH)

    def across_arrived(p, gg, side):
        part = buf.at[p * group + gg, side]
        pltpu.make_async_remote_copy(
            src_ref=part, dst_ref=part,
            send_sem=in_send.at[p * group + gg, side], recv_sem=in_recv.at[p * group + gg, side],
            device_id={"row": partner}, device_id_type=MESH).wait_recv()

    def forward(p):
        part = buf.at[p * group + g, row]

        def hand(gg):
            @pl.when(gg != g)
            def _():
                for side in range(2):
                    across(part, p, gg, side).start()

        each(0, group, hand)
        across(part, p, g, partner).start()

    rim_copy = pltpu.make_async_remote_copy(
        src_ref=f_hbm.at[pl.ds(tokens - WINDOW, WINDOW)], dst_ref=kv.at[pl.ds(0, WINDOW)],
        send_sem=rim_send, recv_sem=rim_recv,
        device_id={"row": partner}, device_id_type=MESH)

    def up_start(i):
        zz = levels - 1 - i

        @pl.when(zz > z)
        def _():
            up(zz).start()

    each(0, levels - 1, up_start)

    def hand_own(gg):
        @pl.when(gg > g)
        def _():
            for side in range(2):
                across(own, z, gg, side).start()

    each(1, group, hand_own)

    @pl.when(row == 0)
    def _():
        rim_copy.start()

    def stacked(k, j):
        rows = pl.ds(j * WINDOW, WINDOW)
        return jnp.concatenate(
            [q[rows, pl.ds((k * per_kv + i) * HD, HD)] for i in range(per_kv)], axis=0)

    rows = per_kv * WINDOW
    wide = 2 * WINDOW
    ones = jnp.ones((wide, HD), jnp.bfloat16)

    def twice(x):
        return jnp.concatenate([x, x], axis=1)

    def attend(unit, query, keys, values, bias, start):
        scores[unit] = nt_dot(query, keys)
        for r in range(0, rows, CHUNK):
            part = pl.ds(r, CHUNK)
            s = scores[unit, part]
            if bias is not None:
                s = s + bias[pl.ds(r % WINDOW, CHUNK)]
            largest = jnp.maximum(s[:, :HD], s[:, HD:])
            largest = jnp.broadcast_to(jnp.max(largest, axis=1, keepdims=True), (CHUNK, HD))
            if not start:
                before = top[unit, part]
                largest = jnp.maximum(before, largest)
                factor[unit, part] = jnp.exp2((before - largest) * EXP_SCALE)
            top[unit, part] = largest
            rounded[unit, part] = jnp.exp2((s - twice(largest)) * EXP_SCALE).astype(jnp.bfloat16)
        fresh = jnp.dot(rounded[unit], values, preferred_element_type=jnp.float32)
        if start:
            acc[unit] = fresh
        else:
            for r in range(0, rows, CHUNK):
                part = pl.ds(r, CHUNK)
                acc[unit, part] = acc[unit, part] * twice(factor[unit, part]) + fresh[r:r + CHUNK]

    t = lax.broadcasted_iota(jnp.int32, (WINDOW, wide), 0)
    s = lax.broadcasted_iota(jnp.int32, (WINDOW, wide), 1)
    near = (s > t) & (s <= t + WINDOW)
    near_bias[1] = jnp.where(near, 0.0, LOW)
    near_bias[0] = jnp.where(near & (s >= jnp.where(row == 0, WINDOW, 0)), 0.0, LOW)

    def local(k, j):
        span = pl.ds(j * WINDOW, wide)
        keys = kv[span, pl.ds(k * HD, HD)]
        values = jnp.concatenate([kv[span, pl.ds(kw + k * HD, HD)], ones], axis=1)
        attend(k * blocks + j, stacked(k, j), keys, values, near_bias.at[min(j, 1)], True)

    load_f.wait()
    load_q.wait()
    load_len.wait()
    for k in range(KVH):
        for j in range(1, blocks):
            local(k, j)

    def relay(back):
        @pl.when(z >= back)
        def _():
            up_arrived(z - back)
            forward(z - back)

    relay(1)

    @pl.when(row == 1)
    def _():
        rim_copy.wait_recv()

    for k in range(KVH):
        local(k, 0)

    each(2, levels, relay)

    first = (lax.broadcasted_iota(jnp.int32, (rows, HD), 1) == 0).astype(jnp.float32).astype(jnp.bfloat16)
    step = wide // slots
    assert slots * step == wide and (step % group == 0 or group % step == 0)

    def remote(piece):
        part = pl.ds(piece * step, step)
        for k in range(KVH):
            keys = buf[part, :, :, pl.ds(k * HD, HD)].reshape(wide, HD)
            values = buf[part, :, :, pl.ds(kw + k * HD, HD)].reshape(wide, HD).astype(jnp.float32)
            dead = values > 1e29
            keys = jnp.concatenate([keys, jnp.where(dead, LOW, 0.0).astype(jnp.bfloat16)], axis=1)
            values = jnp.concatenate([jnp.where(dead, 0.0, values).astype(jnp.bfloat16), ones], axis=1)
            for j in range(blocks):
                query = jnp.concatenate([stacked(k, j), first], axis=1)
                attend(k * blocks + j, query, keys, values, None, False)

    per_piece = max(1, step // group)
    assert levels % per_piece == 0
    pieces = max(1, group // step)

    def take(i):
        high = (levels // per_piece - 1 - i) * per_piece

        @pl.when(high <= z)
        def _():
            def arrive(p):
                @pl.when(p <= z)
                def _():
                    def block(gg):
                        @pl.when((gg != g) & ((p < z) | (gg < g)))
                        def _():
                            for side in range(2):
                                across_arrived(p, gg, side)

                    each(0, group, block)

                @pl.when(p < z)
                def _():
                    across_arrived(p, g, partner)

            for p in reversed(range(per_piece)):
                arrive(high + p)
            if pieces == 1:
                remote(high // per_piece)
            else:
                @pl.loop(0, pieces)
                def _(i):
                    remote(high * pieces + i)

    each(0, levels // per_piece, take)

    for k in range(KVH):
        for j in range(blocks):
            unit = k * blocks + j
            pos = row * tokens + j * WINDOW + lax.broadcasted_iota(jnp.int32, (WINDOW, HD), 0)
            present = pos < len_ref[0]
            for i in range(per_kv):
                part = pl.ds(i * WINDOW, WINDOW)
                result = acc[unit, part, pl.ds(0, HD)] / acc[unit, part, pl.ds(HD, HD)]
                out_ref[pl.ds(j * WINDOW, WINDOW), pl.ds((k * per_kv + i) * HD, HD)] = (
                    jnp.where(present, result, 0.0).astype(out_ref.dtype))

    def up_left(zz):
        @pl.when(zz > z)
        def _():
            up(zz).wait_send()

    each(1, levels, up_left)

    def left_own(gg):
        @pl.when(gg > g)
        def _():
            for side in range(2):
                across(own, z, gg, side).wait_send()

    each(1, group, left_own)

    def left(p):
        @pl.when(p < z)
        def _():
            part = buf.at[p * group + g, row]

            def gone(gg):
                @pl.when(gg != g)
                def _():
                    for side in range(2):
                        across(part, p, gg, side).wait_send()

            each(0, group, gone)
            across(part, p, g, partner).wait_send()

    each(0, levels - 1, left)

    @pl.when(row == 0)
    def _():
        rim_copy.wait_send()


def shards(clips, queries, frames_kv, summary_kv, lengths, caps):
    tokens, width = queries.shape[1:]
    half, kv_width = summary_kv.shape[1:]
    heads = width // HD
    group = 1
    while group * group * 4 <= clips and clips % (group * 2) == 0:
        group *= 2
    levels = clips // group
    units = KVH * (tokens // WINDOW)
    rows = heads // KVH * WINDOW
    dma = pltpu.SemaphoreType.DMA
    anywhere = pl.BlockSpec(memory_space=pl.ANY)
    out = pl.pallas_call(
        functools.partial(kernel, levels, group, heads),
        out_shape=jax.ShapeDtypeStruct((tokens, width), jnp.bfloat16),
        in_specs=[anywhere] * 3 + [pl.BlockSpec(memory_space=pltpu.HBM)] * 2,
        out_specs=pl.BlockSpec(memory_space=pltpu.VMEM),
        scratch_shapes=[
            pltpu.SMEM((1,), jnp.int32),
            pltpu.SMEM((1,), jnp.int32),
            pltpu.VMEM((tokens, width), jnp.bfloat16),
            pltpu.VMEM((WINDOW + tokens, kv_width), jnp.bfloat16),
            pltpu.VMEM((half, kv_width), jnp.bfloat16),
            pltpu.VMEM((half, kv_width), jnp.bfloat16),
            pltpu.VMEM((clips, 2, half, kv_width), jnp.bfloat16),
            pltpu.VMEM((units, rows, 2 * HD), jnp.float32),
            pltpu.VMEM((units, rows, HD), jnp.float32),
            pltpu.VMEM((units, rows, 2 * WINDOW), jnp.float32),
            pltpu.VMEM((units, rows, 2 * WINDOW), jnp.bfloat16),
            pltpu.VMEM((units, rows, HD), jnp.float32),
            pltpu.VMEM((2, WINDOW, 2 * WINDOW), jnp.float32),
            dma((5,)),
            dma((levels,)), dma((levels,)),
            dma((clips, 2)), dma((clips, 2)),
            dma, dma,
        ],
        compiler_params=pltpu.CompilerParams(
            collective_id=0, has_side_effects=True, vmem_limit_bytes=48 * 2**20),
    )(*[pltpu.with_memory_space_constraint(x[0], pltpu.HBM)
        for x in (queries, frames_kv, summary_kv)], lengths, caps)
    return out[None]


def solution(mesh):
    placed = (
        P("clip", "row", None),
        P("clip", "row", None),
        P("clip", "row", None),
        P("clip"),
        P("clip"),
    )
    return jax.shard_map(
        functools.partial(shards, mesh.shape["clip"]),
        mesh=mesh, in_specs=placed, out_specs=P("clip", "row", None), check_vma=False
    )
```
